256 devices in a mesh: row: 32 (over x, z), col: 8 (over y, core).
Axes of the slice: x: 4, y: 4, z: 8, core: 2. Of those that a mesh axis runs over, the one named last changes fastest.
Arguments:
- momentum: float32 [5120, 13312], P('row', 'col')
- gradient: float32 [5120, 13312], P('row', 'col'), may hold values from -6 to 6
Outputs:
- new_momentum: float32 [5120, 13312], P('row', 'col')
- update: float32 [5120, 13312], P('row', 'col')
The draws below stay inside these ranges and needn't reach their ends.
All inputs are finite; a program needn't handle non-finite values.
Results may differ from the reference program's by a relative error of at most 0.00073.
The reference program's roundings to bfloat16 on the way (of `rounded` and `gram_rounded`) count: a program that leaves them out, or rounds other values in their place, can miss the bound.
Values may be sent and summed in bfloat16 or wider, within the bound.
A program may use at most 64 MiB of HBM per device.

```python
import jax
import jax.numpy as jnp

D = 5120
FF_WIN = 13312


def draw_momentum(key, part):
    noise_key = jax.random.fold_in(key, 11)
    return jax.random.normal(noise_key, (D, FF_WIN), jnp.float32)


def steps_of(rng, extent, pieces, least, largest):
    gain, own = 1.0, jax.random.fold_in(rng, 6)
    for axis_at, parts in pieces:
        heights = jnp.exp(jax.random.uniform(jax.random.fold_in(own, axis_at), (parts,), jnp.float32, least / len(pieces), largest / len(pieces)))
        gain = gain * jnp.repeat(heights, extent[axis_at] // parts).reshape([-1 if axis == axis_at else 1 for axis in range(len(extent))])
    return gain


def bell_draw(own_key, extent, width, bound, cuts=(), held_as=jnp.bfloat16):
    factor_of = steps_of(own_key, extent, cuts, -0.22, 0.18) if cuts else 1.0
    array = jax.random.normal(own_key, extent, jnp.float32) * width * factor_of
    return jnp.minimum(jnp.maximum(array, -bound), bound).astype(held_as)


def setup_inputs(seed: int = 0) -> dict:
    key_of = jax.random.split(jax.random.key(seed), 3)
    return {
        "momentum": draw_momentum(jax.random.fold_in(key_of[2], 71), 0),
        "gradient": bell_draw(key_of[1], (D, FF_WIN), 0.5, 6.0, ((0, 32), (1, 8)), jnp.float32),
    }


def reference(momentum, gradient):
    new_momentum = 0.95 * momentum + gradient
    squares = jnp.sum(new_momentum * new_momentum)
    normed = new_momentum / (jnp.sqrt(3.0 * squares / D) + 1e-07)
    rounded = normed.astype(jnp.bfloat16)
    gram = jnp.dot(rounded, rounded.T, preferred_element_type=jnp.float32)
    gram_rounded = gram.astype(jnp.bfloat16)
    product = jnp.dot(gram_rounded, rounded, preferred_element_type=jnp.float32)
    update = (1.5 * normed - 0.5 * product) * jnp.sqrt(jnp.float32(3 * FF_WIN))
    return (new_momentum, update)
```

```python
import functools

import jax
import jax.numpy as jnp
from jax import lax
from jax.experimental import pallas as pl
from jax.experimental.pallas import tpu as pltpu
from jax.sharding import Mesh
from jax.sharding import PartitionSpec as P

D = 5120
FF_WIN = 13312
ROW = ("row_0", "row_1")
COL = ("col_0", "col_1")
X, Z, Y, CORE = 4, 8, 4, 2
ROWS, COLS = D // (X * Z), FF_WIN // (Y * CORE)
HALF = ROWS // 2
A_ROWS, B_ROWS = X * ROWS, Z * ROWS
F32, BF16 = jnp.float32, jnp.bfloat16
GAIN = (3 * FF_WIN) ** 0.5
Z_UP = (0, 1, 3, 5, 7)
Z_DOWN = (0, 2, 4, 6, 7)
X_UP = (0, 1, 3)
X_DOWN = (0, 2, 3)
COLS_X = 1152
COLS_Z = COLS - COLS_X
STEPS = tuple((at, min(256, COLS_X - at)) for at in range(0, COLS_X, 256))


def kernel(
    nm_ref, update_ref,
    tiles, early, early_z, early_x, rb, ra, gt, from_core, half, y_send, y_recv, y_wide, gf, ga, u, u_send, u_mid, u_recv, w, w_send, w_recv,
    done, tile_recv, e_recv, z_recv, x_recv, g_recv, u_rsem, w_rsem,
):
    x, z = lax.axis_index("row_0"), lax.axis_index("row_1")
    y, core = lax.axis_index("col_0"), lax.axis_index("col_1")
    def copy_to(src, dst, send_sem, recv_sem, **where):
        return pltpu.make_async_remote_copy(
            src_ref=src, dst_ref=dst, send_sem=send_sem, recv_sem=recv_sem,
            device_id=where, device_id_type=pl.DeviceIdType.MESH,
        )

    def send(*args, **where):
        copy_to(*args, **where).start()

    def arrive(dst, recv_sem):
        copy_to(dst, dst, recv_sem, recv_sem, col_1=1 - core).wait_recv()

    def sent(src, send_sem):
        copy_to(src, src, send_sem, send_sem, col_1=1 - core).wait_send()

    line_z = [dict(row_1=lax.rem(z + d, Z)) for d in range(1, Z)]
    line_x = [dict(row_0=lax.rem(x + d, X)) for d in range(1, X)]
    column = y * CORE + core
    line_c = []
    for d in range(1, Y * CORE):
        other = lax.rem(column + d, Y * CORE)
        line_c.append(dict(col_0=other // CORE, col_1=lax.rem(other, CORE)))
    partners = line_z + line_x + line_c

    barrier = pltpu.get_barrier_semaphore()
    for where in partners:
        pl.semaphore_signal(barrier, inc=1, device_id=where, device_id_type=pl.DeviceIdType.MESH)

    def add_square(i, total):
        rows = nm_ref[pl.ds(pl.multiple_of(i * 8, 8), 8), :]
        return total + rows * rows

    by_lane = lax.fori_loop(0, ROWS // 8, add_square, jnp.zeros((8, COLS), F32))
    tile = by_lane[:, 0:128]
    for at in range(128, COLS, 128):
        tile = tile + by_lane[:, at : at + 128]
    tile = jnp.sum(tile, axis=0, keepdims=True)
    pl.semaphore_wait(barrier, len(partners))

    up_z, down_z = dict(row_1=lax.rem(z + 1, Z)), dict(row_1=lax.rem(z + Z - 1, Z))
    up_x, down_x = dict(row_0=lax.rem(x + 1, X)), dict(row_0=lax.rem(x + X - 1, X))

    base = 0
    for stage, (me, line, size) in enumerate(((z, line_z, Z), (x, line_x, X), (column, line_c, Y * CORE))):
        tiles[base + me] = tile
        for where in line:
            send(tiles.at[base + me], tiles.at[base + me], done.at[0], tile_recv.at[stage], **where)
        if stage == 0:
            for chunk in range(2):
                for at in range(0, HALF, 16):
                    value = nm_ref[chunk * HALF + at : chunk * HALF + at + 16, :]
                    high = value.astype(BF16)
                    early[chunk, 0, at : at + 16, :] = high
                    early[chunk, 1, at : at + 16, :] = (value - high.astype(F32)).astype(BF16)
            for flow in range(2):
                send(early.at[flow], early_z.at[flow], done.at[1], e_recv.at[0, flow], **(down_z, up_z)[flow])
        if stage == 1:
            for flow in range(2):
                send(early.at[flow], early_x.at[flow], done.at[10], e_recv.at[1, flow], **(down_x, up_x)[flow])
        arrive(tiles.at[pl.ds(base, size - 1)], tile_recv.at[stage])
        tile = tiles[base]
        for k in range(1, size):
            tile = tile + tiles[base + k]
        base += size

    squares = jnp.sum(tile, axis=1, keepdims=True)
    scale = jnp.sqrt(3.0 * squares / D) + 1e-07

    def cast_rows(i, _):
        at = pl.ds(pl.multiple_of(i * 16, 16), 16)
        rounded = (nm_ref[at, :] / scale).astype(BF16)
        rb[at, :] = rounded
        ra[at, :] = rounded
        return 0

    lax.fori_loop(0, ROWS // 16, cast_rows, 0)

    def part(ref, slot, chunk):
        return ref.at[pl.ds(slot * ROWS + chunk * HALF, HALF), :]

    def z_hop(flow, k, chunk):
        slots = (Z_UP, Z_DOWN)[flow]
        send(
            part(rb, slots[k - 1], chunk), part(rb, slots[k], chunk),
            done.at[2], z_recv.at[flow, k - 1, chunk], **(down_z, up_z)[flow],
        )

    def x_hop(flow, k, chunk):
        slots = (X_UP, X_DOWN)[flow]
        send(
            part(ra, slots[k - 1], chunk), part(ra, slots[k], chunk),
            done.at[3], x_recv.at[flow, k - 1, chunk], **(down_x, up_x)[flow],
        )

    def join(pair, ref, slot, chunk):
        for at in range(0, HALF, 16):
            value = pair[0, at : at + 16, :].astype(F32) + pair[1, at : at + 16, :].astype(F32)
            begin = slot * ROWS + chunk * HALF + at
            ref[begin : begin + 16, :] = (value / scale).astype(BF16)

    def z_in(flow, k, chunk):
        slot = (Z_UP, Z_DOWN)[flow][k]
        if k == 1 and chunk == flow:
            arrive(early_z.at[flow], e_recv.at[0, flow])
            join(early_z.at[flow], rb, slot, chunk)
        else:
            arrive(part(rb, slot, chunk), z_recv.at[flow, k - 1, chunk])
        if k < 3 or (k == 3 and chunk == flow):
            z_hop(flow, k + 1, chunk)

    def x_in(flow, k, chunk):
        slot = (X_UP, X_DOWN)[flow][k]
        if k == 1 and chunk == flow:
            arrive(early_x.at[flow], e_recv.at[1, flow])
            join(early_x.at[flow], ra, slot, chunk)
            x_hop(flow, 2, chunk)
        else:
            arrive(part(ra, slot, chunk), x_recv.at[flow, k - 1, chunk])

    y_first, y_second = y + 1 - 2 * lax.rem(y, 2), 3 - y
    mine, theirs = core * HALF, (1 - core) * HALF

    def half_of(ref, slot, which):
        return ref.at[pl.ds(pl.multiple_of(slot * ROWS + which, HALF), HALF), :]

    def gram(low, high):
        left = rb[low * ROWS : high * ROWS, :]
        for at in range(0, A_ROWS, 128):
            gt[low * ROWS : high * ROWS, at : at + 128] = lax.dot_general(
                left, ra[at : at + 128, :], (((1,), (1,)), ((), ())), preferred_element_type=F32
            )
        for slot in range(low, high):
            send(half_of(gt, slot, theirs), from_core.at[slot], done.at[4], g_recv.at[0, slot], col_1=1 - core)

    def y_parts(slot):
        split = HALF // 2 if slot == 0 else 48
        return ((0, split, (y_first, y_second)), (split, HALF - split, (y_second, y_first)))

    def y_send_of(slot, step):
        for at, count, order in y_parts(slot):
            if slot == 0:
                src, dst = half.at[8 * step, pl.ds(at, count), :], y_wide.at[step, pl.ds(at, count), :]
            else:
                src, dst = y_send.at[step, slot, pl.ds(at, count), :], y_recv.at[step, slot, pl.ds(at, count), :]
            send(src, dst, done.at[5 if slot == 0 else 6], g_recv.at[1 + step, slot], col_0=order[step])

    def y_arrive(slot, step):
        arrive(y_wide.at[step] if slot == 0 else y_recv.at[step, slot], g_recv.at[1 + step, slot])

    def sum_cores(slot):
        arrive(from_core.at[slot], g_recv.at[0, slot])
        value = half_of(gt, slot, mine)[...] + from_core[slot]
        half[slot] = value
        if slot:
            y_send[0, slot] = value
        y_send_of(slot, 0)

    def sum_first(slot):
        y_arrive(slot, 0)
        if slot == 0:
            half[8] = half[0] + y_wide[0]
        else:
            value = half[slot] + y_recv[0, slot]
            half[slot] = value
            y_send[1, slot] = value
        y_send_of(slot, 1)

    def sum_second(slot):
        y_arrive(slot, 1)
        if slot == 0:
            value = half[8] + y_wide[1]
        else:
            value = half[slot] + y_recv[1, slot]
        half_of(gf, slot, mine)[...] = value.astype(BF16)
        send(half_of(gf, slot, mine), half_of(gf, slot, mine), done.at[7], g_recv.at[3, slot], col_1=1 - core)

    def turn(slot):
        arrive(half_of(gf, slot, theirs), g_recv.at[3, slot])
        ga[slot] = gf[slot * ROWS : (slot + 1) * ROWS, :].T

    def multiply_z(low, high):
        rows = slice(low * ROWS, high * ROWS)
        w[rows, :] = jnp.dot(gf[rows, :], ra[:, COLS_X:], preferred_element_type=F32)

    def multiply(low, high, first):
        for at, width in STEPS:
            total = None if first else u[:, at : at + width]
            for slot in range(low, high):
                term = jnp.dot(
                    ga[slot], rb[slot * ROWS : (slot + 1) * ROWS, at : at + width], preferred_element_type=F32
                )
                total = term if total is None else total + term
            u[:, at : at + width] = total

    def w_at(flow, chunk, step):
        return flow * 7 + (step if chunk == flow else 3 + step)

    def w_hop(flow, chunk, step):
        begin = (Z_UP, Z_DOWN)[flow][4 - step] * ROWS + chunk * HALF
        value = w[begin : begin + HALF, :]
        at = w_at(flow, chunk, step)
        if step > (0 if chunk == flow else 1):
            arrive(w_recv.at[at - 1], w_rsem.at[flow, chunk, step - 1])
            value = value + w_recv[at - 1]
        w_send[at] = value
        send(w_send.at[at], w_recv.at[at], done.at[9], w_rsem.at[flow, chunk, step], **(up_z, down_z)[flow])

    for flow in range(2):
        z_hop(flow, 1, 1 - flow)
        x_hop(flow, 1, 1 - flow)
    for flow in range(2):
        z_in(flow, 1, flow)
    for flow in range(2):
        x_in(flow, 1, flow)
    for flow in range(2):
        z_in(flow, 1, 1 - flow)
    for flow in range(2):
        x_in(flow, 1, 1 - flow)
    for flow in range(2):
        z_in(flow, 2, flow)
    for flow in range(2):
        x_in(flow, 2, flow)
    gram(0, 1)
    gram(1, 3)
    sum_cores(0)
    for flow in range(2):
        z_in(flow, 2, 1 - flow)
    gram(3, 5)
    sum_cores(1)
    sum_cores(2)
    sum_first(0)
    sum_cores(3)
    sum_cores(4)
    for flow in range(2):
        z_in(flow, 3, flow)
    sum_first(1)
    sum_first(2)
    for flow in range(2):
        z_in(flow, 3, 1 - flow)
    gram(5, 7)
    sum_first(3)
    sum_first(4)
    sum_cores(5)
    sum_cores(6)
    sum_second(0)
    sum_second(1)
    sum_second(2)
    for flow in range(2):
        z_in(flow, 4, flow)
    gram(7, 8)
    sum_cores(7)
    sum_first(5)
    sum_first(6)
    sum_second(3)
    sum_second(4)
    turn(0)
    turn(1)
    turn(2)
    multiply(0, 2, True)
    multiply_z(0, 3)
    sum_first(7)
    turn(3)
    turn(4)
    multiply(2, 5, False)
    multiply_z(3, 5)
    sum_second(5)
    sum_second(6)
    sum_second(7)
    turn(5)
    turn(6)
    multiply_z(5, 7)
    for flow in range(2):
        w_hop(flow, 1 - flow, 1)
    turn(7)

    def u_rows(slot, chunk):
        return u[slot * ROWS + chunk * HALF : slot * ROWS + (chunk + 1) * HALF, :]

    def finish(slot):
        rows = slice(slot * ROWS, (slot + 1) * ROWS)
        total = u[rows, :]
        for late in range(5, Z):
            right = rb[late * ROWS : (late + 1) * ROWS, :COLS_X]
            total = total + jnp.dot(ga[late, rows, :], right, preferred_element_type=F32)
        u[rows, :] = total

    finish(3)
    for flow in range(2):
        u_send[2 * flow] = u_rows(3, flow)
        send(u_send.at[2 * flow], u_mid.at[flow], done.at[8], u_rsem.at[flow, 0], **(up_x, down_x)[flow])
    multiply_z(7, 8)
    for flow in range(2):
        w_hop(flow, flow, 0)
    for flow in range(2):
        finish(1 + flow)
        u_send[2 * flow + 1] = u_rows(1 + flow, 1 - flow)
        send(
            u_send.at[2 * flow + 1], u_recv.at[flow, 1 - flow],
            done.at[8], u_rsem.at[flow, 1], **(up_x, down_x)[flow],
        )
    for flow in range(2):
        w_hop(flow, 1 - flow, 2)
    for flow in range(2):
        w_hop(flow, flow, 1)
    finish(0)
    update_ref[:, :COLS_X] = 1.5 * (nm_ref[:, :COLS_X] / scale) - 0.5 * u[0:ROWS, :]
    update_ref[:, COLS_X:] = 1.5 * (nm_ref[:, COLS_X:] / scale) - 0.5 * w[0:ROWS, :]
    for flow in range(2):
        arrive(u_mid.at[flow], u_rsem.at[flow, 0])
        u_send[4 + flow] = u_rows(1 + flow, flow) + u_mid[flow]
        send(
            u_send.at[4 + flow], u_recv.at[flow, flow],
            done.at[8], u_rsem.at[flow, 2], **(up_x, down_x)[flow],
        )
    for flow in range(2):
        w_hop(flow, 1 - flow, 3)
    for flow in range(2):
        w_hop(flow, flow, 2)
    for flow in range(2):
        w_hop(flow, flow, 3)
    for flow in range(2):
        arrive(u_recv.at[flow, 1 - flow], u_rsem.at[flow, 1])
    for chunk in range(2):
        rows = slice(chunk * HALF, (chunk + 1) * HALF)
        others = jnp.zeros((HALF, COLS_Z), F32)
        for flow in range(2):
            arrive(w_recv.at[w_at(flow, chunk, 3)], w_rsem.at[flow, chunk, 3])
            others = others + w_recv[w_at(flow, chunk, 3)]
        update_ref[rows, COLS_X:] = (update_ref[rows, COLS_X:] - 0.5 * others) * GAIN
    for flow in range(2):
        arrive(u_recv.at[flow, flow], u_rsem.at[flow, 2])
    for chunk in range(2):
        rows = slice(chunk * HALF, (chunk + 1) * HALF)
        others = u_recv[0, chunk] + u_recv[1, chunk]
        update_ref[rows, :COLS_X] = (update_ref[rows, :COLS_X] - 0.5 * others) * GAIN

    for group, src in enumerate((
        tiles.at[pl.ds(0, len(partners))], early, rb.at[pl.ds(0, 12 * HALF), :], ra.at[pl.ds(0, 4 * HALF), :],
        from_core, y_wide, y_send.at[:, pl.ds(1, Z - 1)], gf.at[pl.ds(0, Z * HALF), :], u_send, w_send, early,
    )):
        sent(src, done.at[group])


def products(new_momentum):
    dma = pltpu.SemaphoreType.DMA
    return pl.pallas_call(
        kernel,
        out_shape=pltpu.VMEM((ROWS, COLS), F32),
        in_specs=[pl.BlockSpec(memory_space=pltpu.VMEM)],
        out_specs=pl.BlockSpec(memory_space=pltpu.VMEM),
        scratch_shapes=[
            pltpu.VMEM((Z + X + Y * CORE, 1, 128), F32),
            pltpu.VMEM((2, 2, HALF, COLS), BF16),
            pltpu.VMEM((2, 2, HALF, COLS), BF16),
            pltpu.VMEM((2, 2, HALF, COLS), BF16),
            pltpu.VMEM((B_ROWS, COLS), BF16),
            pltpu.VMEM((A_ROWS, COLS), BF16),
            pltpu.VMEM((B_ROWS, A_ROWS), F32),
            pltpu.VMEM((Z, HALF, A_ROWS), F32),
            pltpu.VMEM((Z + 1, HALF, A_ROWS), F32),
            pltpu.VMEM((2, Z, HALF, A_ROWS), F32),
            pltpu.VMEM((2, Z, HALF, A_ROWS), F32),
            pltpu.VMEM((2, HALF, A_ROWS), F32),
            pltpu.VMEM((B_ROWS, A_ROWS), BF16),
            pltpu.VMEM((Z, A_ROWS, ROWS), BF16),
            pltpu.VMEM((A_ROWS, COLS_X), F32),
            pltpu.VMEM((6, HALF, COLS_X), F32),
            pltpu.VMEM((2, HALF, COLS_X), F32),
            pltpu.VMEM((2, 2, HALF, COLS_X), F32),
            pltpu.VMEM((B_ROWS, COLS_Z), F32),
            pltpu.VMEM((14, HALF, COLS_Z), F32),
            pltpu.VMEM((14, HALF, COLS_Z), F32),
            dma((11,)), dma((3,)), dma((2, 2)), dma((2, 4, 2)), dma((2, 2, 2)), dma((4, Z)), dma((2, 3)), dma((2, 2, 4)),
        ],
        compiler_params=pltpu.CompilerParams(
            collective_id=0, has_side_effects=True, vmem_limit_bytes=56 * 1024 * 1024
        ),
    )(pltpu.with_memory_space_constraint(new_momentum, pltpu.VMEM))


def shards(momentum, gradient):
    new_momentum = 0.95 * momentum + gradient
    update = products(new_momentum)
    return (new_momentum, update)


def solution(mesh):
    torus = Mesh(mesh.devices.reshape(X, Z, Y, CORE), ROW + COL)
    return jax.shard_map(
        shards,
        mesh=torus,
        in_specs=(P(ROW, COL), P(ROW, COL)),
        out_specs=(P(ROW, COL), P(ROW, COL)),
        check_vma=False,
    )
```
